32 devices in a mesh: row: 8 (over y, x, core), col: 4 (over z).
Axes of the slice: x: 2, y: 2, z: 4, core: 2. Of those that a mesh axis runs over, the one named last changes fastest.
Arguments:
- cotangent: bfloat16 [256, 256, 128], P('row', 'col'), may hold values from -6 to 6
- activations: bfloat16 [3, 256, 256, 128], P(None, 'row', 'col'), may hold values from 0 to 2
- active_masks: int32 [3, 256, 256, 128], P(None, 'row', 'col'), may hold values 0 or 1
- weights: bfloat16 [3, 9, 128, 128], replicated, may hold values from -0.1875 to 0.1875
Outputs:
- data_gradient: bfloat16 [256, 256, 128], P('row', 'col')
- weight_gradients: float32 [3, 9, 128, 128], replicated
The draws below stay inside these ranges and needn't reach their ends.
All inputs are finite; a program needn't handle non-finite values. No bound on the sum of `active_masks` on one device may be relied on, other than what follows from the above.
Results may differ from the reference program's by a relative error of at most 0.0054.
Values may be sent and summed in bfloat16 or wider, within the bound.
A program may use at most 64 MiB of HBM per device.

```python
import jax
import jax.numpy as jnp

C = 128
BLOCKS = 3
N = 256


def plant(drawn, own_key, low, top_value):
    extent = drawn.shape
    place = [jax.random.randint(jax.random.fold_in(own_key, axis), (), 0, extent[axis]) for axis in range(len(extent))]
    drawn = drawn.at[tuple(place)].set(low)
    longest = extent.index(max(extent))
    place[longest] = (place[longest] + 1) % extent[longest]
    return drawn.at[tuple(place)].set(top_value)


def shard_levels(rng, extent, pieces, smallest, top_value):
    def one(position, blocks):
        heights = jax.random.uniform(jax.random.fold_in(jax.random.fold_in(rng, 6), position), (blocks,), jnp.float32, smallest / len(pieces), top_value / len(pieces))
        return jnp.repeat(jnp.exp(heights), extent[position] // blocks).reshape((-1,) + (1,) * (len(extent) - position - 1))

    gain = one(*pieces[0])
    for cut in pieces[1:]:
        gain = gain * one(*cut)
    return gain


def scatter_about(own_key, extent, spread, most, pieces=(), kind=jnp.bfloat16):
    gain = shard_levels(own_key, extent, pieces, -0.22, 0.18) if pieces else 1.0
    entries = jax.random.normal(own_key, extent, jnp.float32) * spread * gain
    return jnp.minimum(jnp.maximum(entries, -most), most).astype(kind)


def setup_inputs(seed: int = 0) -> dict:
    streams_of = jax.random.split(jax.random.key(seed), 5)
    cotangent = scatter_about(streams_of[0], (N, N, C), 1.0, 6.0, ((0, 8), (1, 4)))
    activations = jnp.clip(2.0 * jax.random.uniform(streams_of[1], (BLOCKS, N, N, C), jnp.float32) ** shard_levels(streams_of[1], (BLOCKS, N, N, C), ((1, 8), (2, 4)), -0.2, 0.2), 0.0, 2.0).astype(jnp.bfloat16)
    active_masks = plant((jax.random.randint(streams_of[2], (BLOCKS, N, N, C), 0, 2) < 1).astype(jnp.int32), jax.random.fold_in(streams_of[2], 1), 0, 1)
    weights = scatter_about(streams_of[3], (BLOCKS, 9, C, C), (9 * C) ** -0.5, 0.1875)
    return dict(cotangent=cotangent, activations=activations, active_masks=active_masks, weights=weights)


def reference(cotangent, activations, active_masks, weights):
    gradient = cotangent
    results = []
    for layer_index in reversed(range(BLOCKS)):
        dilation = 2 ** layer_index
        mask_now = active_masks[layer_index] > 0
        inputs_now = jnp.where(mask_now, activations[layer_index], jnp.zeros_like(activations[layer_index]))
        wide = gradient.astype(jnp.float32)
        symmetric = ((wide + jnp.transpose(wide, (1, 0, 2))) * 0.5).astype(jnp.bfloat16)
        padded = jnp.pad(symmetric, ((dilation, dilation), (dilation, dilation), (0, 0)))
        flat_inputs = inputs_now.reshape(-1, C)
        accumulated = jnp.zeros((N * N, C), jnp.float32)
        kernel_terms = []
        for tap_down in range(3):
            for tap_across in range(3):
                tap_index = 3 * tap_down + tap_across
                start_down = dilation * (2 - tap_down)
                start_across = dilation * (2 - tap_across)
                shifted = padded[start_down:start_down + N, start_across:start_across + N]
                flat_shift = shifted.reshape(-1, C)
                weight_term = jnp.dot(flat_inputs.T, flat_shift, preferred_element_type=jnp.float32) / N
                kernel_terms.append(weight_term)
                accumulated = accumulated + jnp.dot(flat_shift, weights[layer_index, tap_index].T, preferred_element_type=jnp.float32)
        results.append(jnp.stack(kernel_terms))
        input_change = accumulated.reshape(N, N, C)
        gradient = (gradient.astype(jnp.float32) + jnp.where(mask_now, input_change, jnp.float32(0.0))).astype(jnp.bfloat16)
    weight_gradients = jnp.stack(results[::-1])
    return gradient, weight_gradients
```

```python
import functools

import jax
import jax.numpy as jnp
from jax import lax
from jax.experimental import pallas as pl
from jax.experimental.pallas import tpu as pltpu
from jax.sharding import PartitionSpec as P

MESH = pl.DeviceIdType.MESH
VMEM = pl.BlockSpec(memory_space=pltpu.VMEM)
LATE = True


def remote(src, dst, send, recv, row, col):
    return pltpu.make_async_remote_copy(
        src_ref=src,
        dst_ref=dst,
        send_sem=send,
        recv_sem=recv,
        device_id=(row, col),
        device_id_type=MESH,
    )


def exchange_kernel(chips, cols, g, arrived, relay, send_a, recv_a, send_b, recv_b):
    row, col = lax.axis_index("row"), lax.axis_index("col")
    chip, core = lax.div(row, 2), lax.rem(row, 2)
    height, extent, _ = g.shape
    half = extent // 2
    part = height // chips
    barrier = pltpu.get_barrier_semaphore()

    def first_target(b):
        return (2 * b + core, chip) if LATE else (2 * b + core, col)

    def first_source(k):
        return (2 * col + core, k) if LATE else (2 * k + core, col)

    def second_target(k, h):
        return (2 * k + h, col) if LATE else (2 * col + h, k)

    def second_source(b, h):
        return (2 * b + h, col) if LATE else (2 * b + h, chip)

    def other(place):
        return jnp.logical_or(place[0] != row, place[1] != col)

    def signal(place):
        @pl.when(other(place))
        def _():
            pl.semaphore_signal(barrier, inc=1, device_id=place, device_id_type=MESH)

    for k in range(chips):
        signal(first_source(k))
        for h in range(2):
            signal(second_source(k, h))
    expected = jnp.int32(0)
    for k in range(chips):
        expected += other(first_target(k)).astype(jnp.int32)
        for h in range(2):
            expected += other(second_target(k, h)).astype(jnp.int32)
    pl.semaphore_wait(barrier, expected)

    slot = col if LATE else chip

    def first(b):
        place = first_target(b)
        src = g.at[pl.ds(b * part, part)]
        return place, src, relay.at[slot], send_a.at[b], recv_a.at[slot]

    def second(k, h):
        place = second_target(k, h)
        src = relay.at[k, :, pl.ds(h * half, half)]
        dst = arrived.at[pl.ds(core * height + chip * part, part)]
        return place, src, dst, send_b.at[2 * k + h], recv_b.at[row]

    def begin(item):
        place, src, dst, send, recv = item
        away = other(place)

        @pl.when(away)
        def _():
            remote(src, dst, send, recv, *place).start()

        @pl.when(jnp.logical_not(away))
        def _():
            pltpu.make_async_copy(src, dst, recv).start()

    def finish(item):
        place, src, dst, send, recv = item

        @pl.when(other(place))
        def _():
            remote(src, dst, send, recv, *place).wait_send()

    for b in range(chips):
        begin(first(b))
    for k in range(chips):
        pltpu.make_async_copy(relay.at[k], relay.at[k], recv_a.at[k]).wait()
        for h in range(2):
            begin(second(k, h))
    for b in range(chips):
        finish(first(b))
        for h in range(2):
            finish(second(b, h))
    for b in range(chips):
        for h in range(2):
            dst = arrived.at[pl.ds(h * height + b * part, part)]
            pltpu.make_async_copy(dst, dst, recv_b.at[2 * b + h]).wait()


def exchanged(gradient, index):
    height, extent, channels = gradient.shape
    rows, cols = lax.axis_size("row"), lax.axis_size("col")
    chips = rows // 2
    return pl.pallas_call(
        functools.partial(exchange_kernel, chips, cols),
        out_shape=jax.ShapeDtypeStruct((extent, height, channels), gradient.dtype),
        in_specs=[VMEM],
        out_specs=VMEM,
        scratch_shapes=[
            pltpu.VMEM((chips, height // chips, extent, channels), gradient.dtype),
            pltpu.SemaphoreType.DMA((chips,)),
            pltpu.SemaphoreType.DMA((chips,)),
            pltpu.SemaphoreType.DMA((rows,)),
            pltpu.SemaphoreType.DMA((rows,)),
        ],
        compiler_params=pltpu.CompilerParams(
            collective_id=index, has_side_effects=True
        ),
    )(gradient)


SIDES = [(-1, -1), (-1, 0), (-1, 1), (0, -1), (0, 1), (1, -1), (1, 0), (1, 1)]


def halo_kernel(rows, cols, *refs):
    sources, targets, (send, recv) = refs[:8], refs[8:16], refs[16:]
    row, col = lax.axis_index("row"), lax.axis_index("col")
    barrier = pltpu.get_barrier_semaphore()

    def there(step):
        down, across = row + step[0], col + step[1]
        inside = jnp.logical_and(
            jnp.logical_and(down >= 0, down < rows),
            jnp.logical_and(across >= 0, across < cols),
        )
        return inside, down, across

    expected = jnp.int32(0)
    for step in SIDES:
        inside, down, across = there(step)
        expected += inside.astype(jnp.int32)

        @pl.when(inside)
        def _():
            pl.semaphore_signal(
                barrier, inc=1, device_id=(down, across), device_id_type=MESH
            )

    pl.semaphore_wait(barrier, expected)
    for n, step in enumerate(SIDES):
        inside, down, across = there(step)

        @pl.when(inside)
        def _():
            remote(sources[n], targets[7 - n], send.at[n], recv.at[7 - n], down, across).start()

        @pl.when(jnp.logical_not(inside))
        def _():
            targets[n][...] = jnp.zeros_like(targets[n])

    for n, step in enumerate(SIDES):
        inside, down, across = there(step)

        @pl.when(inside)
        def _():
            remote(sources[n], targets[n], send.at[n], recv.at[n], down, across).wait()


def padded_symmetric(symmetric, d, index):
    height, extent, _ = symmetric.shape
    low, high = slice(0, d), slice(-d, None)
    down = {-1: low, 0: slice(None), 1: high}
    pieces = []
    for y, x in SIDES:
        piece = symmetric[down[y], down[x]]
        pieces.append(jnp.transpose(piece, (1, 0, 2)) if y == 0 else piece)
    got = pl.pallas_call(
        functools.partial(halo_kernel, lax.axis_size("row"), lax.axis_size("col")),
        out_shape=[jax.ShapeDtypeStruct(p.shape, p.dtype) for p in pieces],
        in_specs=[VMEM] * 8,
        out_specs=[VMEM] * 8,
        scratch_shapes=[pltpu.SemaphoreType.DMA((8,)), pltpu.SemaphoreType.DMA((8,))],
        compiler_params=pltpu.CompilerParams(
            collective_id=index, has_side_effects=True
        ),
    )(*pieces)
    left = jnp.transpose(got[3], (1, 0, 2))
    right = jnp.transpose(got[4], (1, 0, 2))
    top = jnp.concatenate([got[0], got[1], got[2]], axis=1)
    middle = jnp.concatenate([left, symmetric, right], axis=1)
    bottom = jnp.concatenate([got[5], got[6], got[7]], axis=1)
    return jnp.concatenate([top, middle, bottom], axis=0)


def reduce_kernel(
    layers, chips, cols, x, out, r1, s1, r2, s2, r3, send1, recv1, send2, recv2, send3, recv3,
    send4, recv4, send5, recv5, send6, recv6,
):
    row, col = lax.axis_index("row"), lax.axis_index("col")
    chip, core = lax.div(row, 2), lax.rem(row, 2)
    sibling = 2 * chip + 1 - core
    wide = jnp.float32

    def chip_at(j):
        return lax.rem(chip + j, chips)

    def col_at(j):
        return lax.rem(col + j, cols)

    barrier = pltpu.get_barrier_semaphore()
    pl.semaphore_signal(barrier, inc=1, device_id=(sibling, col), device_id_type=MESH)
    for j in range(1, chips):
        pl.semaphore_signal(
            barrier, inc=1, device_id=(2 * chip_at(j) + core, col), device_id_type=MESH
        )
    for j in range(1, cols):
        pl.semaphore_signal(barrier, inc=1, device_id=(row, col_at(j)), device_id_type=MESH)
    pl.semaphore_wait(barrier, chips + cols - 1)

    def p1(l):
        return remote(x.at[l, 1 - core], r1.at[l], send1.at[l], recv1.at[l], sibling, col)

    def p2(l, j):
        k = chip_at(j)
        return remote(s1.at[l, k], r2.at[l, j], send2.at[l, j], recv2.at[l, j], 2 * k + core, col)

    def p3(l, j):
        k = col_at(j)
        return remote(s2.at[l, k], r3.at[l, j], send3.at[l, j], recv3.at[l, j], row, k)

    def p4(l, j):
        mine = out.at[l, core, chip, col]
        return remote(mine, mine, send4.at[l, j], recv4.at[l, j], row, col_at(j))

    def p5(l, j):
        mine = out.at[l, core, chip]
        return remote(mine, mine, send5.at[l, j], recv5.at[l, j], 2 * chip_at(j) + core, col)

    def p6(l):
        mine = out.at[l, core]
        return remote(mine, mine, send6.at[l], recv6.at[l], sibling, col)

    for l in range(layers):
        p1(l).start()
    for l in range(layers):
        p1(l).wait_recv()
        s1[l] = (x[l, core].astype(wide) + r1[l].astype(wide)).astype(s1.dtype)
        for j in range(1, chips):
            p2(l, j).start()
    for l in range(layers):
        total = s1[l, chip].astype(wide)
        for j in range(1, chips):
            p2(l, j).wait_recv()
            total += r2[l, j].astype(wide)
        s2[l] = total.astype(s2.dtype)
        for j in range(1, cols):
            p3(l, j).start()
    for l in range(layers):
        total = s2[l, col].astype(wide)
        for j in range(1, cols):
            p3(l, j).wait_recv()
            total += r3[l, j].astype(wide)
        out[l, core, chip, col] = total.astype(out.dtype)
        for j in range(1, cols):
            p4(l, j).start()
    for l in range(layers):
        for j in range(1, cols):
            p4(l, j).wait_recv()
        for j in range(1, chips):
            p5(l, j).start()
    for l in range(layers):
        for j in range(1, chips):
            p5(l, j).wait_recv()
        p6(l).start()
    for l in range(layers):
        p6(l).wait_recv()
        p1(l).wait_send()
        p6(l).wait_send()
        for j in range(1, chips):
            p2(l, j).wait_send()
            p5(l, j).wait_send()
        for j in range(1, cols):
            p3(l, j).wait_send()
            p4(l, j).wait_send()


def reduced(partial, index):
    layers, taps, channels, lanes = partial.shape
    chips, cols = lax.axis_size("row") // 2, lax.axis_size("col")
    count = taps * channels // (2 * chips * cols)
    kind = jnp.bfloat16
    x = partial.astype(kind).reshape(layers, 2, chips, cols, count, lanes)
    dma = pltpu.SemaphoreType.DMA
    out = pl.pallas_call(
        functools.partial(reduce_kernel, layers, chips, cols),
        out_shape=jax.ShapeDtypeStruct(x.shape, kind),
        in_specs=[VMEM],
        out_specs=VMEM,
        scratch_shapes=[
            pltpu.VMEM((layers, chips, cols, count, lanes), kind),
            pltpu.VMEM((layers, chips, cols, count, lanes), kind),
            pltpu.VMEM((layers, chips, cols, count, lanes), kind),
            pltpu.VMEM((layers, cols, count, lanes), kind),
            pltpu.VMEM((layers, cols, count, lanes), kind),
            dma((layers,)), dma((layers,)),
            dma((layers, chips)), dma((layers, chips)),
            dma((layers, cols)), dma((layers, cols)),
            dma((layers, cols)), dma((layers, cols)),
            dma((layers, chips)), dma((layers, chips)),
            dma((layers,)), dma((layers,)),
        ],
        compiler_params=pltpu.CompilerParams(
            collective_id=index, has_side_effects=True
        ),
    )(x)
    return out.reshape(layers, taps, channels, lanes).astype(jnp.float32)


def tap_columns(padded, height, extent, dilation):
    pieces = []
    for tap_down in range(3):
        for tap_across in range(3):
            start_down = dilation * (2 - tap_down)
            start_across = dilation * (2 - tap_across)
            pieces.append(
                padded[start_down : start_down + height, start_across : start_across + extent]
            )
    return jnp.stack(pieces, axis=2)


def per_device(cotangent, activations, active_masks, weights):
    height, extent, channels = cotangent.shape
    map_side = height * lax.axis_size("row")
    layers = weights.shape[0]
    gradient = cotangent
    collected = []
    for layer_index in reversed(range(layers)):
        dilation = 2**layer_index
        mask_now = active_masks[layer_index] > 0
        inputs_now = jnp.where(
            mask_now, activations[layer_index], jnp.zeros_like(activations[layer_index])
        )
        mirror = jnp.transpose(exchanged(gradient, 1 + layer_index), (1, 0, 2))
        symmetric = ((gradient.astype(jnp.float32) + mirror.astype(jnp.float32)) * 0.5).astype(
            jnp.bfloat16
        )
        padded = padded_symmetric(symmetric, dilation, 1 + layers + layer_index)
        stacked = tap_columns(padded, height, extent, dilation)
        partial_value = (
            jnp.einsum("yxi,yxko->kio", inputs_now, stacked, preferred_element_type=jnp.float32)
            / map_side
        )
        input_change = jnp.einsum(
            "yxko,kio->yxi", stacked, weights[layer_index], preferred_element_type=jnp.float32
        )
        gradient = (
            gradient.astype(jnp.float32) + jnp.where(mask_now, input_change, jnp.float32(0.0))
        ).astype(jnp.bfloat16)
        collected.append(partial_value)
    kernel_stack = reduced(jnp.stack(collected[::-1]), 1 + 2 * layers)
    return (gradient, kernel_stack)


def solution(mesh):
    in_specs = (
        P("row", "col", None),
        P(None, "row", "col", None),
        P(None, "row", "col", None),
        P(),
    )
    out_specs = (P("row", "col", None), P())
    return jax.shard_map(
        per_device, mesh=mesh, in_specs=in_specs, out_specs=out_specs, check_vma=False
    )
```

```python
import functools

import jax
import jax.numpy as jnp
from jax import lax
from jax.experimental import pallas as pl
from jax.experimental.pallas import tpu as pltpu
from jax.sharding import PartitionSpec as P

MESH = pl.DeviceIdType.MESH
VMEM = pl.BlockSpec(memory_space=pltpu.VMEM)

def remote(src, dst, send, recv, row, col):
    return pltpu.make_async_remote_copy(
        src_ref=src,
        dst_ref=dst,
        send_sem=send,
        recv_sem=recv,
        device_id=(row, col),
        device_id_type=MESH,
    )


def exchange_kernel(count, chips, cols, *refs):
    fields, arrived = refs[:count], refs[count : 2 * count]
    relay, send_a, recv_a, send_b, recv_b = refs[2 * count :]
    row, col = lax.axis_index("row"), lax.axis_index("col")
    chip, core = lax.div(row, 2), lax.rem(row, 2)
    height, extent, _ = fields[0].shape
    half = extent // 2
    part = height // chips
    barrier = pltpu.get_barrier_semaphore()

    def other(place):
        return jnp.logical_or(place[0] != row, place[1] != col)

    def signal(place):
        @pl.when(other(place))
        def _():
            pl.semaphore_signal(barrier, inc=1, device_id=place, device_id_type=MESH)

    def first_place(j):
        return 2 * lax.rem(chip + j, chips) + core, col

    def second_place(j, h):
        return 2 * col + h, lax.rem(col + j, cols)

    for k in range(chips):
        signal((2 * k + core, col))
        for h in range(2):
            signal((2 * k + h, chip))
    expected = jnp.int32(0)
    for j in range(chips):
        expected += other(first_place(j)).astype(jnp.int32)
        for h in range(2):
            expected += other(second_place(j, h)).astype(jnp.int32)
    pl.semaphore_wait(barrier, expected)

    def first(t, j):
        place = first_place(j)
        src = fields[t].at[pl.ds(lax.rem(chip + j, chips) * part, part)]
        return place, src, relay.at[t, chip], send_a.at[t, j], recv_a.at[t, chip]

    def second(t, j, h):
        place = second_place(j, h)
        src = relay.at[t, place[1], :, pl.ds(h * half, half)]
        dst = arrived[t].at[pl.ds(core * height + chip * part, part)]
        return place, src, dst, send_b.at[t, 2 * j + h], recv_b.at[t, row]

    def begin(item):
        place, src, dst, send, recv = item
        away = other(place)

        @pl.when(away)
        def _():
            remote(src, dst, send, recv, *place).start()

        @pl.when(jnp.logical_not(away))
        def _():
            pltpu.make_async_copy(src, dst, recv).start()

    def finish(item):
        place, src, dst, send, recv = item

        @pl.when(other(place))
        def _():
            remote(src, dst, send, recv, *place).wait_send()

    for t in range(count):
        for j in range(chips):
            begin(first(t, j))
    for t in range(count):
        for j in range(cols):
            k = lax.rem(col + j, cols)
            slab = relay.at[t, k]
            pltpu.make_async_copy(slab, slab, recv_a.at[t, k]).wait()
            for h in range(2):
                begin(second(t, j, h))
    for t in range(count):
        for j in range(chips):
            finish(first(t, j))
            for h in range(2):
                finish(second(t, j, h))
    for t in range(count):
        for b in range(chips):
            for h in range(2):
                dst = arrived[t].at[pl.ds(h * height + b * part, part)]
                pltpu.make_async_copy(dst, dst, recv_b.at[t, 2 * b + h]).wait()


def mirrored(fields, index):
    height, extent, channels = fields[0].shape
    kind = fields[0].dtype
    rows, cols = lax.axis_size("row"), lax.axis_size("col")
    chips, count = rows // 2, len(fields)
    dma = pltpu.SemaphoreType.DMA
    got = pl.pallas_call(
        functools.partial(exchange_kernel, count, chips, cols),
        out_shape=[jax.ShapeDtypeStruct((extent, height, channels), kind)] * count,
        in_specs=[VMEM] * count,
        out_specs=[VMEM] * count,
        scratch_shapes=[
            pltpu.VMEM((count, chips, height // chips, extent, channels), kind),
            dma((count, chips)),
            dma((count, chips)),
            dma((count, rows)),
            dma((count, rows)),
        ],
        compiler_params=pltpu.CompilerParams(
            collective_id=index, has_side_effects=True
        ),
    )(*fields)
    return [jnp.transpose(field, (1, 0, 2)) for field in got]


SIDES = [(-1, -1), (-1, 0), (-1, 1), (0, -1), (0, 1), (1, -1), (1, 0), (1, 1)]


def halo_kernel(rows, cols, *refs):
    sources, targets, (send, recv) = refs[:8], refs[8:16], refs[16:]
    row, col = lax.axis_index("row"), lax.axis_index("col")
    barrier = pltpu.get_barrier_semaphore()

    def there(step):
        down, across = row + step[0], col + step[1]
        inside = jnp.logical_and(
            jnp.logical_and(down >= 0, down < rows),
            jnp.logical_and(across >= 0, across < cols),
        )
        return inside, down, across

    expected = jnp.int32(0)
    for step in SIDES:
        inside, down, across = there(step)
        expected += inside.astype(jnp.int32)

        @pl.when(inside)
        def _():
            pl.semaphore_signal(
                barrier, inc=1, device_id=(down, across), device_id_type=MESH
            )

    pl.semaphore_wait(barrier, expected)
    for n, step in enumerate(SIDES):
        inside, down, across = there(step)

        @pl.when(inside)
        def _():
            remote(sources[n], targets[7 - n], send.at[n], recv.at[7 - n], down, across).start()

        @pl.when(jnp.logical_not(inside))
        def _():
            targets[n][...] = jnp.zeros_like(targets[n])

    for n, step in enumerate(SIDES):
        inside, down, across = there(step)

        @pl.when(inside)
        def _():
            remote(sources[n], targets[n], send.at[n], recv.at[n], down, across).wait()


def padded_symmetric(symmetric, d, index):
    height, extent, _ = symmetric.shape
    low, high = slice(0, d), slice(-d, None)
    down = {-1: low, 0: slice(None), 1: high}
    pieces = []
    for y, x in SIDES:
        piece = symmetric[down[y], down[x]]
        pieces.append(jnp.transpose(piece, (1, 0, 2)) if y == 0 else piece)
    got = pl.pallas_call(
        functools.partial(halo_kernel, lax.axis_size("row"), lax.axis_size("col")),
        out_shape=[jax.ShapeDtypeStruct(p.shape, p.dtype) for p in pieces],
        in_specs=[VMEM] * 8,
        out_specs=[VMEM] * 8,
        scratch_shapes=[pltpu.SemaphoreType.DMA((8,)), pltpu.SemaphoreType.DMA((8,))],
        compiler_params=pltpu.CompilerParams(
            collective_id=index, has_side_effects=True
        ),
    )(*pieces)
    left = jnp.transpose(got[3], (1, 0, 2))
    right = jnp.transpose(got[4], (1, 0, 2))
    top = jnp.concatenate([got[0], got[1], got[2]], axis=1)
    middle = jnp.concatenate([left, symmetric, right], axis=1)
    bottom = jnp.concatenate([got[5], got[6], got[7]], axis=1)
    return jnp.concatenate([top, middle, bottom], axis=0)


def reduce_kernel(
    layers, chips, cols, x, out, r1, s1, r2, s2, r3, send1, recv1, send2, recv2, send3, recv3,
    send4, recv4, send5, recv5, send6, recv6,
):
    row, col = lax.axis_index("row"), lax.axis_index("col")
    chip, core = lax.div(row, 2), lax.rem(row, 2)
    sibling = 2 * chip + 1 - core
    wide = jnp.float32

    def chip_at(j):
        return lax.rem(chip + j, chips)

    def col_at(j):
        return lax.rem(col + j, cols)

    barrier = pltpu.get_barrier_semaphore()
    pl.semaphore_signal(barrier, inc=1, device_id=(sibling, col), device_id_type=MESH)
    for j in range(1, chips):
        pl.semaphore_signal(
            barrier, inc=1, device_id=(2 * chip_at(j) + core, col), device_id_type=MESH
        )
    for j in range(1, cols):
        pl.semaphore_signal(barrier, inc=1, device_id=(row, col_at(j)), device_id_type=MESH)
    pl.semaphore_wait(barrier, chips + cols - 1)

    def p1(l):
        return remote(x.at[l, 1 - core], r1.at[l], send1.at[l], recv1.at[l], sibling, col)

    def p2(l, j):
        k = chip_at(j)
        return remote(s1.at[l, k], r2.at[l, j], send2.at[l, j], recv2.at[l, j], 2 * k + core, col)

    def p3(l, j):
        k = col_at(j)
        return remote(s2.at[l, k], r3.at[l, j], send3.at[l, j], recv3.at[l, j], row, k)

    def p4(l, j):
        mine = out.at[l, core, chip, col]
        return remote(mine, mine, send4.at[l, j], recv4.at[l, j], row, col_at(j))

    def p5(l, j):
        mine = out.at[l, core, chip]
        return remote(mine, mine, send5.at[l, j], recv5.at[l, j], 2 * chip_at(j) + core, col)

    def p6(l):
        mine = out.at[l, core]
        return remote(mine, mine, send6.at[l], recv6.at[l], sibling, col)

    for l in range(layers):
        p1(l).start()
    for l in range(layers):
        p1(l).wait_recv()
        s1[l] = (x[l, core].astype(wide) + r1[l].astype(wide)).astype(s1.dtype)
        for j in range(1, chips):
            p2(l, j).start()
    for l in range(layers):
        total = s1[l, chip].astype(wide)
        for j in range(1, chips):
            p2(l, j).wait_recv()
            total += r2[l, j].astype(wide)
        s2[l] = total.astype(s2.dtype)
        for j in range(1, cols):
            p3(l, j).start()
    for l in range(layers):
        total = s2[l, col].astype(wide)
        for j in range(1, cols):
            p3(l, j).wait_recv()
            total += r3[l, j].astype(wide)
        out[l, core, chip, col] = total.astype(out.dtype)
        for j in range(1, cols):
            p4(l, j).start()
    for l in range(layers):
        for j in range(1, cols):
            p4(l, j).wait_recv()
        for j in range(1, chips):
            p5(l, j).start()
    for l in range(layers):
        for j in range(1, chips):
            p5(l, j).wait_recv()
        p6(l).start()
    for l in range(layers):
        p6(l).wait_recv()
        p1(l).wait_send()
        p6(l).wait_send()
        for j in range(1, chips):
            p2(l, j).wait_send()
            p5(l, j).wait_send()
        for j in range(1, cols):
            p3(l, j).wait_send()
            p4(l, j).wait_send()


def reduced(partial, index):
    layers, taps, channels, lanes = partial.shape
    chips, cols = lax.axis_size("row") // 2, lax.axis_size("col")
    count = taps * channels // (2 * chips * cols)
    kind = jnp.bfloat16
    x = partial.astype(kind).reshape(layers, 2, chips, cols, count, lanes)
    dma = pltpu.SemaphoreType.DMA
    out = pl.pallas_call(
        functools.partial(reduce_kernel, layers, chips, cols),
        out_shape=jax.ShapeDtypeStruct(x.shape, kind),
        in_specs=[VMEM],
        out_specs=VMEM,
        scratch_shapes=[
            pltpu.VMEM((layers, chips, cols, count, lanes), kind),
            pltpu.VMEM((layers, chips, cols, count, lanes), kind),
            pltpu.VMEM((layers, chips, cols, count, lanes), kind),
            pltpu.VMEM((layers, cols, count, lanes), kind),
            pltpu.VMEM((layers, cols, count, lanes), kind),
            dma((layers,)), dma((layers,)),
            dma((layers, chips)), dma((layers, chips)),
            dma((layers, cols)), dma((layers, cols)),
            dma((layers, cols)), dma((layers, cols)),
            dma((layers, chips)), dma((layers, chips)),
            dma((layers,)), dma((layers,)),
        ],
        compiler_params=pltpu.CompilerParams(
            collective_id=index, has_side_effects=True
        ),
    )(x)
    return out.reshape(layers, taps, channels, lanes).astype(jnp.float32)


def tap_columns(padded, height, extent, dilation):
    pieces = []
    for tap_down in range(3):
        for tap_across in range(3):
            start_down = dilation * (2 - tap_down)
            start_across = dilation * (2 - tap_across)
            pieces.append(
                padded[start_down : start_down + height, start_across : start_across + extent]
            )
    return jnp.stack(pieces, axis=2)


def per_device(cotangent, activations, active_masks, weights):
    height, extent, channels = cotangent.shape
    map_side = height * lax.axis_size("row")
    layers = weights.shape[0]
    wide = jnp.float32
    masks = [active_masks[n] > 0 for n in range(layers)]
    fields = [cotangent] + [masks[n].astype(cotangent.dtype) for n in range(layers - 1, 0, -1)]
    mirrors = mirrored(fields, 1)
    gradient, opposite = cotangent, mirrors[0]
    collected = []
    for layer_index in reversed(range(layers)):
        dilation = 2**layer_index
        mask_now = masks[layer_index]
        inputs_now = jnp.where(
            mask_now, activations[layer_index], jnp.zeros_like(activations[layer_index])
        )
        symmetric = ((gradient.astype(wide) + opposite.astype(wide)) * 0.5).astype(jnp.bfloat16)
        padded = padded_symmetric(symmetric, dilation, 2 + layer_index)
        stacked = tap_columns(padded, height, extent, dilation)
        kernels = weights[layer_index]
        if layer_index:
            swapped = kernels.reshape(3, 3, channels, channels).swapaxes(0, 1)
            kernels = jnp.concatenate([kernels, swapped.reshape(9, channels, channels)], axis=1)
        change = jnp.einsum("yxko,kio->yxi", stacked, kernels, preferred_element_type=wide)
        partial_value = (
            jnp.einsum("yxi,yxko->kio", inputs_now, stacked, preferred_element_type=wide)
            / map_side
        )
        gradient = (
            gradient.astype(wide) + jnp.where(mask_now, change[..., :channels], wide(0.0))
        ).astype(jnp.bfloat16)
        if layer_index:
            mask_there = mirrors[layers - layer_index] > 0
            opposite = (
                opposite.astype(wide) + jnp.where(mask_there, change[..., channels:], wide(0.0))
            ).astype(jnp.bfloat16)
        collected.append(partial_value)
    kernel_stack = reduced(jnp.stack(collected[::-1]), 2 + layers)
    return (gradient, kernel_stack)


def solution(mesh):
    in_specs = (
        P("row", "col", None),
        P(None, "row", "col", None),
        P(None, "row", "col", None),
        P(),
    )
    out_specs = (P("row", "col", None), P())
    return jax.shard_map(
        per_device, mesh=mesh, in_specs=in_specs, out_specs=out_specs, check_vma=False
    )
```

```python
import functools

import jax
import jax.numpy as jnp
from jax import lax
from jax.experimental import pallas as pl
from jax.experimental.pallas import tpu as pltpu
from jax.sharding import PartitionSpec as P

MESH = pl.DeviceIdType.MESH
VMEM = pl.BlockSpec(memory_space=pltpu.VMEM)
WIDE = jnp.float32
NARROW = jnp.bfloat16
EDGE = 16
CHUNK = 8
SIDES = [(-1, -1), (-1, 0), (-1, 1), (0, -1), (0, 1), (1, -1), (1, 0), (1, 1)]


def remote(src, dst, send, recv, row, col):
    return pltpu.make_async_remote_copy(
        src_ref=src,
        dst_ref=dst,
        send_sem=send,
        recv_sem=recv,
        device_id=(row, col),
        device_id_type=MESH,
    )


def whole_kernel(layers, rows, cols, share, slab, *refs):
    cotangent, activations, masks, kernels, gradient, total = refs[:6]
    (
        fields, relay, arrived, opposite, there, padded, shifted, x, r1, s1, r2, s2, r3, z,
        send_a, recv_a, send_b, recv_b, send_h, recv_h, send1, recv1, send2, recv2,
        send3, recv3, send4, recv4, send5, recv5, send6, recv6,
    ) = refs[6:]
    chips = rows // 2
    row, col = lax.axis_index("row"), lax.axis_index("col")
    chip, core = lax.div(row, 2), lax.rem(row, 2)
    sibling = 2 * chip + 1 - core
    height, extent, channels = cotangent.shape
    half, part = extent // 2, height // chips
    rim = (padded.shape[1] - height) // 2
    side = height * rows
    breadth = extent + 2 * EDGE

    @pl.loop(0, height // CHUNK)
    def _(n):
        at = pl.ds(n * CHUNK, CHUNK)
        for t in range(layers - 1):
            fields[t, at] = masks[layers - 1 - t, at].astype(WIDE).astype(NARROW)

    padded[...] = jnp.zeros_like(padded)
    s2[...] = jnp.zeros_like(s2)
    x[...] = jnp.zeros_like(x)

    barrier = pltpu.get_barrier_semaphore()

    @pl.loop(0, rows)
    def _(r):
        for c in range(cols):

            @pl.when(jnp.logical_or(r != row, c != col))
            def _():
                pl.semaphore_signal(barrier, inc=1, device_id=(r, c), device_id_type=MESH)

    pl.semaphore_wait(barrier, rows * cols - 1)

    def other(place):
        return jnp.logical_or(place[0] != row, place[1] != col)

    def first(t, j):
        b = lax.rem(chip + j, chips)
        field = cotangent if t == 0 else fields.at[t - 1]
        src = field.at[pl.ds(b * part, part)]
        return (2 * b + core, col), src, relay.at[t, chip], send_a.at[t, j], recv_a.at[t, chip]

    def second(t, j, h):
        k = lax.rem(col + j, cols)
        src = relay.at[t, k, :, pl.ds(h * half, half)]
        dst = arrived.at[t, pl.ds(core * height + chip * part, part)]
        return (2 * col + h, k), src, dst, send_b.at[t, 2 * j + h], recv_b.at[t, row]

    def begin(item):
        place, src, dst, send, recv = item
        away = other(place)

        @pl.when(away)
        def _():
            remote(src, dst, send, recv, *place).start()

        @pl.when(jnp.logical_not(away))
        def _():
            pltpu.make_async_copy(src, dst, recv).start()

    def finish(item):
        place, src, dst, send, recv = item

        @pl.when(other(place))
        def _():
            remote(src, dst, send, recv, *place).wait_send()

    def forward(t):
        for j in range(cols):
            k = lax.rem(col + j, cols)
            pltpu.make_async_copy(relay.at[t, k], relay.at[t, k], recv_a.at[t, k]).wait()
            for h in range(2):
                begin(second(t, j, h))

    def collect(t, result):
        for b in range(chips):
            for h in range(2):
                dst = arrived.at[t, pl.ds(h * height + b * part, part)]
                pltpu.make_async_copy(dst, dst, recv_b.at[t, 2 * b + h]).wait()

        @pl.loop(0, extent // 16)
        def _(n):
            at = pl.ds(pl.multiple_of(n * 16, 16), 16)
            result[:, at] = jnp.swapaxes(arrived[t, at].astype(WIDE), 0, 1).astype(NARROW)

    def place_of(step):
        down, across = row + step[0], col + step[1]
        inside = jnp.logical_and(
            jnp.logical_and(down >= 0, down < rows),
            jnp.logical_and(across >= 0, across < cols),
        )
        return inside, down, across

    def spans(step, d, landing):
        y, w = step
        if landing:
            ys = {-1: (rim - d, d), 0: (rim, height), 1: (rim + height, d)}[y]
            xs = {-1: (0, EDGE), 0: (EDGE, extent), 1: (EDGE + extent, EDGE)}[w]
        else:
            ys = {-1: (rim, d), 0: (rim, height), 1: (rim + height - d, d)}[y]
            xs = {-1: (EDGE, EDGE), 0: (EDGE, extent), 1: (extent, EDGE)}[w]
        return pl.ds(*ys), pl.ds(*xs)

    def halo(l, n, receiver):
        step, d = SIDES[n], 2**l
        inside, down, across = place_of(step)
        src = padded.at[(l,) + spans(step, d, False)]
        if receiver:
            dst = padded.at[(l,) + spans(step, d, True)]
            return inside, remote(src, dst, send_h.at[l, n], recv_h.at[l, n], down, across)
        back = (-step[0], -step[1])
        dst = padded.at[(l,) + spans(back, d, True)]
        return inside, remote(src, dst, send_h.at[l, n], recv_h.at[l, 7 - n], down, across)

    def halo_start(l):
        for n in range(8):
            inside, copy = halo(l, n, False)
            pl.when(inside)(copy.start)

    def halo_wait(l):
        for n in range(8):
            inside, copy = halo(l, n, True)
            pl.when(inside)(copy.wait)

    def symmetrize(l, mine):
        @pl.loop(0, height // CHUNK)
        def _(n):
            at = pl.ds(n * CHUNK, CHUNK)
            both = mine[at].astype(WIDE) + opposite[at].astype(WIDE)
            padded[l, pl.ds(rim + n * CHUNK, CHUNK), pl.ds(EDGE, extent)] = (both * 0.5).astype(
                NARROW
            )

    def shift(l):
        d = 2**l

        @pl.loop(rim - d, rim + height + d)
        def _(r):
            line = padded[l, r].astype(WIDE)
            for b in range(3):
                moved = line
                if b != 1:
                    moved = pltpu.roll(line, (d * (b - 1)) % breadth, 0)
                shifted[l % 2, r, :, b * channels : (b + 1) * channels] = moved[
                    EDGE : EDGE + extent
                ].astype(NARROW)

    def cells(l, a, n):
        start = rim + 2**l * (1 - a) + n * CHUNK
        return shifted[l % 2, pl.ds(start, CHUNK)].reshape(CHUNK * extent, 3 * channels)

    def data(l, mine):
        @pl.loop(0, height // CHUNK)
        def _(n):
            at = pl.ds(n * CHUNK, CHUNK)
            change = jnp.zeros((CHUNK * extent, (2 if l else 1) * channels), WIDE)
            for a in range(3):
                weight = kernels[l, a] if l else kernels[l, a, :, :channels]
                change += jnp.dot(cells(l, a, n), weight, preferred_element_type=WIDE)
            own = change[:, :channels].reshape(CHUNK, extent, channels)
            new = mine[at].astype(WIDE) + jnp.where(masks[l, at] > 0, own, 0.0)
            gradient[at] = new.astype(NARROW)
            if l:
                own = change[:, channels:].reshape(CHUNK, extent, channels)
                open_ = there[at].astype(WIDE) > 0
                new = opposite[at].astype(WIDE) + jnp.where(open_, own, 0.0)
                opposite[at] = new.astype(NARROW)

    def weight(l):
        for a in range(3):

            @pl.loop(0, height // CHUNK)
            def _(n):
                at = pl.ds(n * CHUNK, CHUNK)
                inputs = jnp.where(masks[l, at] > 0, activations[l, at].astype(WIDE), 0.0)
                inputs = inputs.astype(NARROW).reshape(CHUNK * extent, channels)
                term = lax.dot_general(
                    inputs, cells(l, a, n), (((0,), (0,)), ((), ())), preferred_element_type=WIDE
                ) / side
                for b in range(3):
                    here = pl.ds((3 * a + b) * channels, channels)
                    x[l, here] += term[:, b * channels : (b + 1) * channels]

    def chip_at(j):
        return lax.rem(chip + j, chips)

    def col_at(j):
        return lax.rem(col + j, cols)

    def piece(core_at, k):
        return pl.ds(pl.multiple_of((core_at * chips + k) * share, 16), share)

    def wide_piece(core_at):
        return pl.ds(pl.multiple_of(core_at * chips * share, 16), chips * share)

    def slabs(k):
        return pl.ds(pl.multiple_of(k * slab, 16), slab)

    def p1(l):
        return remote(x.at[l, wide_piece(1 - core)], r1.at[l], send1.at[l], recv1.at[l], sibling, col)

    def p2(l, j):
        k = chip_at(j)
        src = s1.at[l, pl.ds(pl.multiple_of(k * share, 16), share)]
        return remote(src, r2.at[l, j], send2.at[l, j], recv2.at[l, j], 2 * k + core, col)

    def p3(l, j):
        k = col_at(j)
        return remote(s2.at[l, slabs(k)], r3.at[l, j], send3.at[l, j], recv3.at[l, j], row, k)

    def p4(l, j):
        mine = z.at[l, slabs(col)]
        return remote(mine, mine, send4.at[l, j], recv4.at[l, j], row, col_at(j))

    def p5(l, j):
        src, dst = z.at[l, pl.ds(0, share)], total.at[l, piece(core, chip)]
        return remote(src, dst, send5.at[l, j], recv5.at[l, j], 2 * chip_at(j) + core, col)

    def p6(l):
        mine = total.at[l, wide_piece(core)]
        return remote(mine, mine, send6.at[l], recv6.at[l], sibling, col)

    def sum1(l):
        p1(l).start()

    def sum2(l):
        p1(l).wait_recv()
        s1[l] = (x[l, wide_piece(core)] + r1[l]).astype(NARROW)
        for j in range(1, chips):
            p2(l, j).start()

    def sum3(l):
        value = s1[l, pl.ds(pl.multiple_of(chip * share, 16), share)].astype(WIDE)
        for j in range(1, chips):
            p2(l, j).wait_recv()
            value += r2[l, j].astype(WIDE)
        s2[l, pl.ds(0, share)] = value.astype(NARROW)
        for j in range(1, cols):
            p3(l, j).start()

    def sum4(l):
        value = s2[l, slabs(col)].astype(WIDE)
        for j in range(1, cols):
            p3(l, j).wait_recv()
            value += r3[l, j].astype(WIDE)
        z[l, slabs(col)] = value.astype(NARROW)
        for j in range(1, cols):
            p4(l, j).start()

    def sum5(l):
        for j in range(1, cols):
            p4(l, j).wait_recv()
        for j in range(1, chips):
            p5(l, j).start()
        total[l, piece(core, chip)] = z[l, pl.ds(0, share)]

    def sum6(l):
        for j in range(1, chips):
            p5(l, j).wait_recv()
        p6(l).start()

    def sum7(l):
        p6(l).wait_recv()
        p1(l).wait_send()
        p6(l).wait_send()
        for j in range(1, chips):
            p2(l, j).wait_send()
            p5(l, j).wait_send()
        for j in range(1, cols):
            p3(l, j).wait_send()
            p4(l, j).wait_send()

    for t in range(layers):
        for j in range(chips):
            begin(first(t, j))
    forward(0)
    for t in range(1, layers):
        forward(t)
    collect(0, opposite)
    pending = []

    def advance():
        for steps in pending:
            if steps:
                steps.pop(0)()

    top = layers - 1
    for l in range(top, -1, -1):
        mine = cotangent if l == top else gradient
        symmetrize(l, mine)
        halo_start(l)
        if l < top:
            weight(l + 1)
            pending.append([functools.partial(f, l + 1) for f in (sum1, sum2, sum3, sum4, sum5, sum6, sum7)])
        advance()
        halo_wait(l)
        shift(l)
        advance()
        if l:
            collect(top - l + 1, there)
            data(l, mine)
            advance()
    weight(0)
    pending.append([functools.partial(f, 0) for f in (sum1, sum2, sum3, sum4, sum5, sum6, sum7)])
    advance()
    data(0, gradient)
    while any(pending):
        advance()
    for t in range(layers):
        for j in range(chips):
            finish(first(t, j))
            for h in range(2):
                finish(second(t, j, h))


def per_device(cotangent, activations, active_masks, weights):
    height, extent, channels = cotangent.shape
    rows, cols = lax.axis_size("row"), lax.axis_size("col")
    chips = rows // 2
    layers = weights.shape[0]
    rim = 2 ** (layers - 1)
    lines = 9 * channels
    share = pl.cdiv(lines, rows * 16) * 16
    slab = pl.cdiv(share, cols * 16) * 16
    taps = weights.reshape(layers, 3, 3, channels, channels)
    straight = jnp.transpose(taps, (0, 1, 2, 4, 3))
    swapped = jnp.transpose(taps, (0, 2, 1, 4, 3))
    kernels = jnp.concatenate([straight, swapped], axis=-1)
    kernels = kernels.reshape(layers, 3, 3 * channels, 2 * channels)
    dma = pltpu.SemaphoreType.DMA
    gradient, total = pl.pallas_call(
        functools.partial(whole_kernel, layers, rows, cols, share, slab),
        out_shape=[
            jax.ShapeDtypeStruct((height, extent, channels), NARROW),
            jax.ShapeDtypeStruct((layers, rows * share, channels), NARROW),
        ],
        in_specs=[VMEM] * 4,
        out_specs=[VMEM] * 2,
        scratch_shapes=[
            pltpu.VMEM((layers - 1, height, extent, channels), NARROW),
            pltpu.VMEM((layers, chips, height // chips, extent, channels), NARROW),
            pltpu.VMEM((layers, extent, height, channels), NARROW),
            pltpu.VMEM((height, extent, channels), NARROW),
            pltpu.VMEM((height, extent, channels), NARROW),
            pltpu.VMEM((layers, height + 2 * rim, extent + 2 * EDGE, channels), NARROW),
            pltpu.VMEM((2, height + 2 * rim, extent, 3 * channels), NARROW),
            pltpu.VMEM((layers, rows * share, channels), WIDE),
            pltpu.VMEM((layers, chips * share, channels), WIDE),
            pltpu.VMEM((layers, chips * share, channels), NARROW),
            pltpu.VMEM((layers, chips, share, channels), NARROW),
            pltpu.VMEM((layers, cols * slab, channels), NARROW),
            pltpu.VMEM((layers, cols, slab, channels), NARROW),
            pltpu.VMEM((layers, cols * slab, channels), NARROW),
            dma((layers, chips)), dma((layers, chips)),
            dma((layers, rows)), dma((layers, rows)),
            dma((layers, 8)), dma((layers, 8)),
            dma((layers,)), dma((layers,)),
            dma((layers, chips)), dma((layers, chips)),
            dma((layers, cols)), dma((layers, cols)),
            dma((layers, cols)), dma((layers, cols)),
            dma((layers, chips)), dma((layers, chips)),
            dma((layers,)), dma((layers,)),
        ],
        compiler_params=pltpu.CompilerParams(
            collective_id=1, has_side_effects=True, vmem_limit_bytes=60 * 2**20
        ),
    )(cotangent, activations, active_masks, kernels)
    kernel_stack = total[:, :lines].reshape(weights.shape).astype(WIDE)
    return gradient, kernel_stack


def solution(mesh):
    in_specs = (
        P("row", "col", None),
        P(None, "row", "col", None),
        P(None, "row", "col", None),
        P(),
    )
    out_specs = (P("row", "col", None), P())
    return jax.shard_map(
        per_device, mesh=mesh, in_specs=in_specs, out_specs=out_specs, check_vma=False
    )
```

```python
import functools

import jax
import jax.numpy as jnp
from jax import lax
from jax.experimental import pallas as pl
from jax.experimental.pallas import tpu as pltpu
from jax.sharding import PartitionSpec as P

MESH = pl.DeviceIdType.MESH
VMEM = pl.BlockSpec(memory_space=pltpu.VMEM)
WIDE = jnp.float32
NARROW = jnp.bfloat16
EDGE = 16
CHUNK = 8
SIDES = [(-1, -1), (-1, 0), (-1, 1), (0, -1), (0, 1), (1, -1), (1, 0), (1, 1)]


def remote(src, dst, send, recv, row, col):
    return pltpu.make_async_remote_copy(
        src_ref=src,
        dst_ref=dst,
        send_sem=send,
        recv_sem=recv,
        device_id=(row, col),
        device_id_type=MESH,
    )


def whole_kernel(layers, rows, cols, share, slab, *refs):
    cotangent, activations, masks, kernels, gradient, total = refs[:6]
    (
        fields, relay, arrived, opposite, there, padded, shifted, x, r1, s1, r2, s2, r3, z,
        send_a, recv_a, send_b, recv_b, send_h, recv_h, send1, recv1, send2, recv2,
        send3, recv3, send4, recv4, send5, recv5, send6, recv6,
    ) = refs[6:]
    chips = rows // 2
    row, col = lax.axis_index("row"), lax.axis_index("col")
    chip, core = lax.div(row, 2), lax.rem(row, 2)
    sibling = 2 * chip + 1 - core
    height, extent, channels = cotangent.shape
    half, part = extent // 2, height // chips
    rim = (padded.shape[1] - height) // 2
    side = height * rows
    breadth = extent + 2 * EDGE

    @pl.loop(0, height // CHUNK)
    def _(n):
        at = pl.ds(n * CHUNK, CHUNK)
        for t in range(layers - 1):
            fields[t, at] = masks[layers - 1 - t, at].astype(WIDE).astype(NARROW)

    padded[...] = jnp.zeros_like(padded)
    s2[...] = jnp.zeros_like(s2)
    x[...] = jnp.zeros_like(x)

    barrier = pltpu.get_barrier_semaphore()

    @pl.loop(0, rows)
    def _(r):
        for c in range(cols):

            @pl.when(jnp.logical_or(r != row, c != col))
            def _():
                pl.semaphore_signal(barrier, inc=1, device_id=(r, c), device_id_type=MESH)

    pl.semaphore_wait(barrier, rows * cols - 1)

    def other(place):
        return jnp.logical_or(place[0] != row, place[1] != col)

    def first(t, j):
        b = lax.rem(chip + j, chips)
        field = cotangent if t == 0 else fields.at[t - 1]
        src = field.at[pl.ds(b * part, part)]
        return (2 * b + core, col), src, relay.at[t, chip], send_a.at[t, j], recv_a.at[t, chip]

    def second(t, j, h):
        k = lax.rem(col + j, cols)
        src = relay.at[t, k, :, pl.ds(h * half, half)]
        dst = arrived.at[t, pl.ds(core * height + chip * part, part)]
        return (2 * col + h, k), src, dst, send_b.at[t, 2 * j + h], recv_b.at[t, row]

    def begin(item):
        place, src, dst, send, recv = item
        away = other(place)

        @pl.when(away)
        def _():
            remote(src, dst, send, recv, *place).start()

        @pl.when(jnp.logical_not(away))
        def _():
            pltpu.make_async_copy(src, dst, recv).start()

    def finish(item):
        place, src, dst, send, recv = item

        @pl.when(other(place))
        def _():
            remote(src, dst, send, recv, *place).wait_send()

    def forward(t):
        for j in range(cols):
            k = lax.rem(col + j, cols)
            pltpu.make_async_copy(relay.at[t, k], relay.at[t, k], recv_a.at[t, k]).wait()
            for h in range(2):
                begin(second(t, j, h))

    def collect(t, result):
        for b in range(chips):
            for h in range(2):
                dst = arrived.at[t, pl.ds(h * height + b * part, part)]
                pltpu.make_async_copy(dst, dst, recv_b.at[t, 2 * b + h]).wait()

        @pl.loop(0, extent // 16)
        def _(n):
            at = pl.ds(pl.multiple_of(n * 16, 16), 16)
            result[:, at] = jnp.swapaxes(arrived[t, at].astype(WIDE), 0, 1).astype(NARROW)

    def place_of(step):
        down, across = row + step[0], col + step[1]
        inside = jnp.logical_and(
            jnp.logical_and(down >= 0, down < rows),
            jnp.logical_and(across >= 0, across < cols),
        )
        return inside, down, across

    def spans(step, d, landing):
        y, w = step
        if landing:
            ys = {-1: (rim - d, d), 0: (rim, height), 1: (rim + height, d)}[y]
            xs = {-1: (0, EDGE), 0: (EDGE, extent), 1: (EDGE + extent, EDGE)}[w]
        else:
            ys = {-1: (rim, d), 0: (rim, height), 1: (rim + height - d, d)}[y]
            xs = {-1: (EDGE, EDGE), 0: (EDGE, extent), 1: (extent, EDGE)}[w]
        return pl.ds(*ys), pl.ds(*xs)

    def halo(l, n, receiver):
        step, d = SIDES[n], 2**l
        inside, down, across = place_of(step)
        src = padded.at[(l,) + spans(step, d, False)]
        if receiver:
            dst = padded.at[(l,) + spans(step, d, True)]
            return inside, remote(src, dst, send_h.at[l, n], recv_h.at[l, n], down, across)
        back = (-step[0], -step[1])
        dst = padded.at[(l,) + spans(back, d, True)]
        return inside, remote(src, dst, send_h.at[l, n], recv_h.at[l, 7 - n], down, across)

    def halo_start(l):
        for n in range(8):
            inside, copy = halo(l, n, False)
            pl.when(inside)(copy.start)

    def halo_wait(l):
        for n in range(8):
            inside, copy = halo(l, n, True)
            pl.when(inside)(copy.wait)

    def symmetrize(l, mine):
        @pl.loop(0, height // CHUNK)
        def _(n):
            at = pl.ds(n * CHUNK, CHUNK)
            both = mine[at].astype(WIDE) + opposite[at].astype(WIDE)
            padded[l, pl.ds(rim + n * CHUNK, CHUNK), pl.ds(EDGE, extent)] = (both * 0.5).astype(
                NARROW
            )

    def shift(l):
        d = 2**l

        @pl.loop(rim - d, rim + height + d)
        def _(r):
            line = padded[l, r].astype(WIDE)
            for b in range(3):
                moved = line
                if b != 1:
                    moved = pltpu.roll(line, (d * (b - 1)) % breadth, 0)
                shifted[l % 2, r, :, b * channels : (b + 1) * channels] = moved[
                    EDGE : EDGE + extent
                ].astype(NARROW)

    def cells(l, a, n):
        start = rim + 2**l * (1 - a) + n * CHUNK
        return shifted[l % 2, pl.ds(start, CHUNK)].reshape(CHUNK * extent, 3 * channels)

    def against(value, weight):
        return lax.dot_general(
            value, weight, (((1,), (1,)), ((), ())), preferred_element_type=WIDE
        )

    def data(l, mine):
        @pl.loop(0, height // CHUNK)
        def _(n):
            at = pl.ds(n * CHUNK, CHUNK)
            own = jnp.zeros((CHUNK * extent, channels), WIDE)
            flipped = own
            for a in range(3):
                values = cells(l, a, n)
                for b in range(3):
                    value = values[:, b * channels : (b + 1) * channels]
                    own += against(value, kernels[l, 3 * a + b])
                    if l:
                        flipped += against(value, kernels[l, 3 * b + a])
            own = own.reshape(CHUNK, extent, channels)
            new = mine[at].astype(WIDE) + jnp.where(masks[l, at] > 0, own, 0.0)
            gradient[at] = new.astype(NARROW)
            if l:
                own = flipped.reshape(CHUNK, extent, channels)
                open_ = there[at].astype(WIDE) > 0
                new = opposite[at].astype(WIDE) + jnp.where(open_, own, 0.0)
                opposite[at] = new.astype(NARROW)

    def weight(l):
        for a in range(3):

            @pl.loop(0, height // CHUNK)
            def _(n):
                at = pl.ds(n * CHUNK, CHUNK)
                inputs = jnp.where(masks[l, at] > 0, activations[l, at].astype(WIDE), 0.0)
                inputs = inputs.astype(NARROW).reshape(CHUNK * extent, channels)
                term = lax.dot_general(
                    inputs, cells(l, a, n), (((0,), (0,)), ((), ())), preferred_element_type=WIDE
                ) / side
                for b in range(3):
                    here = pl.ds((3 * a + b) * channels, channels)
                    x[l, here] += term[:, b * channels : (b + 1) * channels]

    def chip_at(j):
        return lax.rem(chip + j, chips)

    def col_at(j):
        return lax.rem(col + j, cols)

    def piece(core_at, k):
        return pl.ds(pl.multiple_of((core_at * chips + k) * share, 16), share)

    def wide_piece(core_at):
        return pl.ds(pl.multiple_of(core_at * chips * share, 16), chips * share)

    def slabs(k):
        return pl.ds(pl.multiple_of(k * slab, 16), slab)

    def p1(l):
        return remote(x.at[l, wide_piece(1 - core)], r1.at[l], send1.at[l], recv1.at[l], sibling, col)

    def p2(l, j):
        k = chip_at(j)
        src = s1.at[l, pl.ds(pl.multiple_of(k * share, 16), share)]
        return remote(src, r2.at[l, j], send2.at[l, j], recv2.at[l, j], 2 * k + core, col)

    def p3(l, j):
        k = col_at(j)
        return remote(s2.at[l, slabs(k)], r3.at[l, j], send3.at[l, j], recv3.at[l, j], row, k)

    def p4(l, j):
        mine = z.at[l, slabs(col)]
        return remote(mine, mine, send4.at[l, j], recv4.at[l, j], row, col_at(j))

    def p5(l, j):
        src, dst = z.at[l, pl.ds(0, share)], total.at[l, piece(core, chip)]
        return remote(src, dst, send5.at[l, j], recv5.at[l, j], 2 * chip_at(j) + core, col)

    def p6(l):
        mine = total.at[l, wide_piece(core)]
        return remote(mine, mine, send6.at[l], recv6.at[l], sibling, col)

    def sum1(l):
        p1(l).start()

    def sum2(l):
        p1(l).wait_recv()
        s1[l] = (x[l, wide_piece(core)] + r1[l]).astype(NARROW)
        for j in range(1, chips):
            p2(l, j).start()

    def sum3(l):
        value = s1[l, pl.ds(pl.multiple_of(chip * share, 16), share)].astype(WIDE)
        for j in range(1, chips):
            p2(l, j).wait_recv()
            value += r2[l, j].astype(WIDE)
        s2[l, pl.ds(0, share)] = value.astype(NARROW)
        for j in range(1, cols):
            p3(l, j).start()

    def sum4(l):
        value = s2[l, slabs(col)].astype(WIDE)
        for j in range(1, cols):
            p3(l, j).wait_recv()
            value += r3[l, j].astype(WIDE)
        z[l, slabs(col)] = value.astype(NARROW)
        for j in range(1, cols):
            p4(l, j).start()

    def sum5(l):
        for j in range(1, cols):
            p4(l, j).wait_recv()
        for j in range(1, chips):
            p5(l, j).start()
        total[l, piece(core, chip)] = z[l, pl.ds(0, share)]

    def sum6(l):
        for j in range(1, chips):
            p5(l, j).wait_recv()
        p6(l).start()

    def sum7(l):
        p6(l).wait_recv()
        p1(l).wait_send()
        p6(l).wait_send()
        for j in range(1, chips):
            p2(l, j).wait_send()
            p5(l, j).wait_send()
        for j in range(1, cols):
            p3(l, j).wait_send()
            p4(l, j).wait_send()

    for t in range(layers):
        for j in range(chips):
            begin(first(t, j))
        if t:
            forward(t - 1)
    forward(layers - 1)
    collect(0, opposite)
    pending = []
    SUMS = (sum1, sum2, sum3, sum4, sum5, sum6, sum7)

    def advance():
        for steps in pending:
            if steps:
                steps.pop(0)()

    top = layers - 1
    for l in range(top, -1, -1):
        mine = cotangent if l == top else gradient
        symmetrize(l, mine)
        halo_start(l)
        advance()
        halo_wait(l)
        shift(l)
        weight(l)
        pending.append([functools.partial(f, l) for f in SUMS])
        advance()
        if l:
            collect(top - l + 1, there)
        data(l, mine)
        if l:
            advance()
    while any(pending):
        advance()
    for t in range(layers):
        for j in range(chips):
            finish(first(t, j))
            for h in range(2):
                finish(second(t, j, h))


def per_device(cotangent, activations, active_masks, weights):
    height, extent, channels = cotangent.shape
    rows, cols = lax.axis_size("row"), lax.axis_size("col")
    chips = rows // 2
    layers = weights.shape[0]
    rim = 2 ** (layers - 1)
    lines = 9 * channels
    share = pl.cdiv(lines, rows * 16) * 16
    slab = pl.cdiv(share, cols * 16) * 16
    dma = pltpu.SemaphoreType.DMA
    gradient, total = pl.pallas_call(
        functools.partial(whole_kernel, layers, rows, cols, share, slab),
        out_shape=[
            jax.ShapeDtypeStruct((height, extent, channels), NARROW),
            jax.ShapeDtypeStruct((layers, rows * share, channels), NARROW),
        ],
        in_specs=[VMEM] * 4,
        out_specs=[VMEM] * 2,
        scratch_shapes=[
            pltpu.VMEM((layers - 1, height, extent, channels), NARROW),
            pltpu.VMEM((layers, chips, height // chips, extent, channels), NARROW),
            pltpu.VMEM((layers, extent, height, channels), NARROW),
            pltpu.VMEM((height, extent, channels), NARROW),
            pltpu.VMEM((height, extent, channels), NARROW),
            pltpu.VMEM((layers, height + 2 * rim, extent + 2 * EDGE, channels), NARROW),
            pltpu.VMEM((2, height + 2 * rim, extent, 3 * channels), NARROW),
            pltpu.VMEM((layers, rows * share, channels), WIDE),
            pltpu.VMEM((layers, chips * share, channels), WIDE),
            pltpu.VMEM((layers, chips * share, channels), NARROW),
            pltpu.VMEM((layers, chips, share, channels), NARROW),
            pltpu.VMEM((layers, cols * slab, channels), NARROW),
            pltpu.VMEM((layers, cols, slab, channels), NARROW),
            pltpu.VMEM((layers, cols * slab, channels), NARROW),
            dma((layers, chips)), dma((layers, chips)),
            dma((layers, rows)), dma((layers, rows)),
            dma((layers, 8)), dma((layers, 8)),
            dma((layers,)), dma((layers,)),
            dma((layers, chips)), dma((layers, chips)),
            dma((layers, cols)), dma((layers, cols)),
            dma((layers, cols)), dma((layers, cols)),
            dma((layers, chips)), dma((layers, chips)),
            dma((layers,)), dma((layers,)),
        ],
        compiler_params=pltpu.CompilerParams(
            collective_id=1, has_side_effects=True, vmem_limit_bytes=60 * 2**20
        ),
    )(cotangent, activations, active_masks, weights)
    kernel_stack = total[:, :lines].reshape(weights.shape).astype(WIDE)
    return gradient, kernel_stack


def solution(mesh):
    in_specs = (
        P("row", "col", None),
        P(None, "row", "col", None),
        P(None, "row", "col", None),
        P(),
    )
    out_specs = (P("row", "col", None), P())
    return jax.shard_map(
        per_device, mesh=mesh, in_specs=in_specs, out_specs=out_specs, check_vma=False
    )
```
